128 devices in a mesh: row: 8 (over y, x_hi), col: 16 (over z, x_lo, core).
Axes of the slice: x: 4 (x_hi: 2, x_lo: 2; x = x_hi * 2 + x_lo), y: 4, z: 4, core: 2. Of those that a mesh axis runs over, the one named last changes fastest.
Arguments:
- landmarks: float32 [81920, 128], P(('row', 'col')), may hold values from -6 to 6
- slab_points: float32 [4096, 128], P('col'), may hold values from -6 to 6
- panel_points: float32 [2, 256, 128], replicated, may hold values from -6 to 6, as said below
- inverse_blocks: float32 [2, 256, 256], replicated, as said below
Outputs:
- updated_slab: float32 [81920, 4096], P('row', 'col')
The draws below stay inside these ranges and needn't reach their ends.
Inputs may be any that keep to these rules, and one draw needn't show every extreme that they name: `panel_points`: points of order one, at most 6 in magnitude. inverse_blocks[0] is the inverse of the lower Cholesky factor of gaussian(panel_points[0], panel_points[0]) + 0.001 I; inverse_blocks[1] is the inverse of the lower Cholesky factor of gaussian(panel_points[1], panel_points[1]) - first_next first_next^T + 0.001 I. Both are lower triangular with a positive diagonal.
All inputs are finite; a program needn't handle non-finite values.
Results may differ from the reference program's by a relative error of at most 0.0003.
Values sent between devices are 32-bit elements; how exact they have to be, the bound alone decides.
A program may use at most 128 MiB of HBM per device.

```python
import jax
import jax.numpy as jnp
from jax import lax

DIM = 128
PANEL = 256
ROWS_DEV = 640
LANDMARKS = 81920
SLAB = 4096


def shared_points(key):
    point_key = jax.random.fold_in(key, 4177)
    points = jnp.clip(jax.random.normal(point_key, (2, PANEL, DIM), jnp.float32), -6.0, 6.0)
    return points


def kernel_rows(left_points, right_points):
    inner = lax.dot_general(left_points, right_points, (((1,), (1,)), ((), ())), precision=lax.Precision.HIGHEST, preferred_element_type=jnp.float32)
    left_norms = jnp.sum(left_points * left_points, axis=1)[:, None]
    right_norms = jnp.sum(right_points * right_points, axis=1)[None, :]
    return jnp.exp((2.0 * inner - left_norms - right_norms) / DIM)


def draw_panel_points(key, part):
    return shared_points(key)


def draw_inverse_blocks(key, part):
    points = shared_points(key)
    identity = jnp.eye(PANEL, dtype=jnp.float32)
    first_factor = jnp.linalg.cholesky(kernel_rows(points[0], points[0]) + 0.001 * identity)
    first_inverse = jax.scipy.linalg.solve_triangular(first_factor, identity, lower=True)
    first_next = lax.dot_general(kernel_rows(points[1], points[0]), first_inverse, (((1,), (1,)), ((), ())), precision=lax.Precision.HIGHEST, preferred_element_type=jnp.float32)
    schur_block = kernel_rows(points[1], points[1]) - lax.dot_general(first_next, first_next, (((1,), (1,)), ((), ())), precision=lax.Precision.HIGHEST, preferred_element_type=jnp.float32)
    second_factor = jnp.linalg.cholesky(schur_block + 0.001 * identity)
    second_inverse = jax.scipy.linalg.solve_triangular(second_factor, identity, lower=True)
    return jnp.stack([first_inverse, second_inverse], axis=0)


def steps_of(stream_key, shape, pieces, low, high):
    def one(dim, blocks):
        draws = jax.random.uniform(jax.random.fold_in(jax.random.fold_in(stream_key, 6), dim), (blocks,), jnp.float32, low / len(pieces), high / len(pieces))
        return jnp.repeat(jnp.exp(draws), shape[dim] // blocks).reshape((-1,) + (1,) * (len(shape) - dim - 1))

    loudness = one(*pieces[0])
    for cut in pieces[1:]:
        loudness = loudness * one(*cut)
    return loudness


def normal_values(rng, shape, spread, reach, cuts=(), held_as=jnp.bfloat16):
    drawn = jax.random.normal(rng, shape, jnp.float32) * spread
    if len(cuts) > 0:
        drawn = steps_of(rng, shape, cuts, -0.22, 0.18) * drawn
    return jnp.clip(drawn, min=-reach, max=reach).astype(held_as)


def setup_inputs(seed: int = 0) -> dict:
    key_list = jax.random.split(jax.random.key(seed), 5)
    return {
        "landmarks": normal_values(key_list[0], (LANDMARKS, DIM), 1.0, 6.0, ((0, 128),), jnp.float32),
        "slab_points": normal_values(key_list[1], (SLAB, DIM), 1.0, 6.0, ((0, 16),), jnp.float32),
        "panel_points": draw_panel_points(jax.random.fold_in(key_list[4], 71), 0),
        "inverse_blocks": draw_inverse_blocks(jax.random.fold_in(key_list[4], 71), 0),
    }


def dot_rows(left_matrix, right_matrix):
    return lax.dot_general(left_matrix.astype(jnp.float32), right_matrix.astype(jnp.float32), (((1,), (1,)), ((), ())), precision=lax.Precision.HIGHEST, preferred_element_type=jnp.float32)

def gaussian(left_points, right_points):
    inner = dot_rows(left_points, right_points)
    left_norms = jnp.sum(left_points * left_points, axis=1)[:, None]
    right_norms = jnp.sum(right_points * right_points, axis=1)[None, :]
    return jnp.exp((2.0 * inner - left_norms - right_norms) / left_points.shape[1])

def factors(points, panel_points, inverse_blocks, first_next):
    first_panel = dot_rows(gaussian(points, panel_points[0]), inverse_blocks[0])
    second_raw = gaussian(points, panel_points[1]) - dot_rows(first_panel, first_next)
    second_panel = dot_rows(second_raw, inverse_blocks[1])
    return jnp.concatenate([first_panel, second_panel], axis=1)

def reference(landmarks, slab_points, panel_points, inverse_blocks):
    first_next = dot_rows(gaussian(panel_points[1], panel_points[0]), inverse_blocks[0])
    slab_factors = factors(slab_points, panel_points, inverse_blocks, first_next)
    blocks = landmarks.reshape(-1, ROWS_DEV, DIM)

    def one_block(landmark_block):
        return gaussian(landmark_block, slab_points) - dot_rows(factors(landmark_block, panel_points, inverse_blocks, first_next), slab_factors)
    result = lax.map(one_block, blocks)
    return result.reshape(-1, slab_points.shape[0])
```

```python
import functools
import math

import jax
import jax.numpy as jnp
from jax import lax
from jax.experimental import pallas as pl
from jax.experimental.pallas import tpu as pltpu
from jax.sharding import PartitionSpec as P

MESH = pl.DeviceIdType.MESH
F32, BF16 = jnp.float32, jnp.bfloat16
DIM = 128
PANEL = 256
ROWS = 640
HALF = 320
CHIP = 1280
COLS = 256
SCALE = math.log2(math.e) / DIM

UNITS_A = [
    ((0, 0, 0), (0, 1, 0)),
    ((0, 0, 1), (0, 1, 1)),
    ((4, 0, 0), (3, 0, 0)),
    ((1, 1, 0), (4, 0, 1)),
    ((3, 0, 1), (1, 1, 1)),
    ((4, 1, 0), (3, 1, 0)),
    ((1, 0, 0), (4, 1, 1)),
    ((3, 1, 1), (1, 0, 1)),
    ((2, 0, 0), (2, 1, 0)),
    ((2, 0, 1), (2, 1, 1)),
    ((7, 0, 0), (5, 0, 0)),
    ((7, 0, 1), (5, 0, 1)),
]
UNITS_B = [
    ((6, 0, 0), (6, 0, 1)),
    ((7, 1, 0), (7, 1, 1)),
    ((5, 1, 0), (5, 1, 1)),
    ((6, 1, 0), (6, 1, 1)),
]


def place():
    me = lax.axis_index("col")
    return me // 4, (me // 2) % 2, me % 2


def dot(a, b):
    return lax.dot_general(a, b, (((1,), (0,)), ((), ())), preferred_element_type=F32)


def dot_full(a, b):
    return lax.dot_general(
        a, b, (((1,), (0,)), ((), ())), precision=lax.Precision.HIGHEST, preferred_element_type=F32
    )


def split(v):
    hi = v.astype(BF16)
    return hi, (v - hi.astype(F32)).astype(BF16)


def offset(piece, core):
    _, half, other = piece
    plane = core if other == 0 else 1 - core
    return pl.multiple_of(plane * ROWS + half * HALF, HALF)


def rows_of(held, unit, core):
    return jnp.concatenate([held[p[0], pl.ds(offset(p, core), HALF), :] for p in unit], axis=0)


def kernel_phase(points, we, cs):
    hi, lo = split(points)
    raw = dot(jnp.concatenate([hi, lo, hi], axis=1), we[...])
    panel = jnp.exp2(raw[:, : 2 * PANEL])
    slab = jnp.exp2(raw[:, 2 * PANEL :] + cs[...])
    scale = jnp.exp2(-SCALE * jnp.sum(points * points, axis=1, keepdims=True))
    ghi, glo = split(panel)
    return jnp.concatenate([ghi, glo, ghi], axis=1), slab, scale


def update_phase(phase, mc):
    panel, slab, scale = phase
    return scale * (slab - dot(panel, mc[...]))


def gather_kernel(
    l_ref, s_ref, p_ref, a_ref, held, res, we, mc, cs, s_v, p_v, a_v, send, recv, loc
):
    z, x, core = place()

    def device(dz, dx, dc):
        return {"col": (((z + dz) % 4) * 2 + (x + dx) % 2) * 2 + (core + dc) % 2}

    partner, across, up, down = device(0, 0, 1), device(0, 1, 0), device(1, 0, 0), device(3, 0, 0)
    barrier = pltpu.get_barrier_semaphore()
    for d in (partner, across, up, down):
        pl.semaphore_signal(barrier, inc=1, device_id=d, device_id_type=MESH)
    own_rows = pl.ds(pl.multiple_of(core * ROWS, ROWS), ROWS)
    local = [
        pltpu.make_async_copy(p_ref, p_v, loc.at[0]),
        pltpu.make_async_copy(s_ref, s_v, loc.at[1]),
        pltpu.make_async_copy(a_ref, a_v, loc.at[2]),
        pltpu.make_async_copy(l_ref, held.at[0, own_rows], loc.at[3]),
    ]
    for copy in local:
        copy.start()
    pl.semaphore_wait(barrier, 4)

    sends = []

    def go(src, slot, half, target):
        copy = pltpu.make_async_remote_copy(
            src_ref=src,
            dst_ref=held.at[slot, pl.ds(offset((slot, half, 0), core), HALF)],
            send_sem=send.at[len(sends)],
            recv_sem=recv.at[slot, core, half],
            device_id=target,
            device_id_type=MESH,
        )
        copy.start()
        sends.append(copy)

    def mine(slot, half):
        return held.at[slot, pl.ds(offset((slot, half, 0), core), HALF)]

    def wait(slot, half, other):
        ref = held.at[slot, pl.ds(offset((slot, half, other), core), HALF)]
        plane = core if other == 0 else 1 - core
        pltpu.make_async_copy(ref, ref, recv.at[slot, plane, half]).wait()

    def arrive(slot, half):
        wait(slot, half, 0)
        go(mine(slot, half), slot, half, partner)

    def fetch(slot, halves=(0, 1)):
        for half in halves:
            wait(slot, half, 1)

    for i in (0, 1):
        first, second = l_ref.at[pl.ds(i * HALF, HALF)], l_ref.at[pl.ds((1 - i) * HALF, HALF)]
        go(first, 3, i, up)
        go(second, 1, 1 - i, down)
        go(first, 4, i, across)
        go(first, 0, i, partner)

    local[0].wait()
    local[1].wait()
    panel = p_v[...].reshape(2 * PANEL, DIM)
    turned = jnp.concatenate([panel.T, s_v[...].T], axis=1)
    scaled = turned * (2.0 * SCALE)
    hi, lo = split(scaled)
    we[...] = jnp.concatenate([hi, hi, lo], axis=0)
    columns = -SCALE * jnp.sum(turned * turned, axis=0, keepdims=True)
    cs[...] = columns[:, 2 * PANEL :]
    weights = -SCALE * jnp.sum(panel * panel, axis=1, keepdims=True)
    grid = jnp.exp2(dot_full(panel, scaled[:, 2 * PANEL :]) + weights + columns[:, 2 * PANEL :])
    k0, k1 = grid[:PANEL], grid[PANEL:]
    local[2].wait()
    a0, a1 = a_v[0], a_v[1]
    inv0, inv1 = dot_full(a0.T, a0), dot_full(a1.T, a1)
    g10 = jnp.exp2(dot_full(panel[PANEL:], scaled[:, :PANEL]) + weights[PANEL:] + columns[:, :PANEL])
    qt = dot_full(g10, inv0)
    m1 = dot_full(inv1, k1 - dot_full(qt, k0))
    m0 = dot_full(inv0, k0) - dot_full(qt.T, m1)
    scale_rows = jnp.exp2(weights)
    mhi, mlo = split(jnp.concatenate([m0, m1], axis=0) * scale_rows)
    mc[...] = jnp.concatenate([mhi, mhi, mlo], axis=0)
    local[3].wait()

    pending = []

    def begin(unit):
        pending.append((unit, kernel_phase(rows_of(held, unit, core), we, cs)))

    def finish():
        unit, phase = pending.pop(0)
        out = update_phase(phase, mc)
        for n, piece in enumerate(unit):
            res[piece[0], pl.ds(offset(piece, core), HALF), :] = out[n * HALF : (n + 1) * HALF]

    def before(i):
        if i == 1:
            fetch(0)
        if i == 2:
            arrive(4, 0)
            arrive(3, 0)
            go(mine(3, 0), 2, 0, up)
            arrive(1, 1)
            go(mine(1, 1), 2, 1, down)
            go(mine(4, 0), 7, 0, up)
            go(mine(4, 0), 5, 0, down)
        if i == 3:
            fetch(4, (0,))
        if i == 4:
            fetch(3, (0,))
            fetch(1, (1,))
        if i == 5:
            arrive(4, 1)
            go(mine(4, 1), 7, 1, up)
            go(mine(4, 1), 5, 1, down)
            arrive(3, 1)
            arrive(1, 0)
        if i == 6:
            fetch(4, (1,))
        if i == 7:
            fetch(3, (1,))
            fetch(1, (0,))
        if i == 8:
            arrive(2, 0)
            go(mine(2, 0), 6, 0, across)
            arrive(2, 1)
            go(mine(2, 1), 6, 1, across)
        if i == 9:
            fetch(2)
        if i == 10:
            arrive(7, 0)
            arrive(5, 0)
        if i == 11:
            fetch(7, (0,))
            fetch(5, (0,))

    for i, unit in enumerate(UNITS_A):
        before(i)
        begin(unit)
        if i:
            finish()
    arrive(6, 0)
    finish()
    arrive(7, 1)
    arrive(5, 1)
    arrive(6, 1)
    fetch(6, (0,))
    fetch(7, (1,))
    fetch(5, (1,))
    fetch(6, (1,))
    for copy in sends:
        copy.wait_send()


def finish_kernel(held, res, we, mc, cs, out, last, sems):
    z, x, core = place()

    def target(slot, start, size):
        chip = ((z + slot % 4) % 4) * 2 + (x + slot // 4) % 2
        return out.at[pl.ds(pl.multiple_of(chip * CHIP + start, HALF), size)]

    copies = []

    def put(src, slot, start, size):
        copy = pltpu.make_async_copy(src, target(slot, start, size), sems.at[len(copies)])
        copy.start()
        copies.append(copy)

    for slot in (0, 4, 3, 1, 2):
        put(res.at[slot], slot, 0, CHIP)
    for slot in (7, 5):
        for plane in (0, 1):
            put(res.at[slot, pl.ds(plane * ROWS, HALF)], slot, plane * ROWS, HALF)
    for n, unit in enumerate(UNITS_B):
        phase = kernel_phase(rows_of(held, unit, core), we, cs)
        last[n] = update_phase(phase, mc)
        for m, piece in enumerate(unit):
            put(last.at[n, pl.ds(m * HALF, HALF)], piece[0], offset(piece, core), HALF)
    for copy in copies:
        copy.wait()


def local(landmarks, slab_points, panel_points, inverse_blocks):
    hbm = pl.BlockSpec(memory_space=pl.ANY)
    vmem = pl.BlockSpec(memory_space=pltpu.VMEM)
    held, res, we, mc, cs = pl.pallas_call(
        gather_kernel,
        name="gather",
        in_specs=[hbm] * 4,
        out_specs=[vmem] * 5,
        out_shape=[
            pltpu.VMEM((8, CHIP, DIM), F32),
            pltpu.VMEM((8, CHIP, COLS), F32),
            pltpu.VMEM((3 * DIM, 2 * PANEL + COLS), BF16),
            pltpu.VMEM((6 * PANEL, COLS), BF16),
            pltpu.VMEM((1, COLS), F32),
        ],
        scratch_shapes=[
            pltpu.VMEM((COLS, DIM), F32),
            pltpu.VMEM((2, PANEL, DIM), F32),
            pltpu.VMEM((2, PANEL, PANEL), F32),
            pltpu.SemaphoreType.DMA((64,)),
            pltpu.SemaphoreType.DMA((8, 2, 2)),
            pltpu.SemaphoreType.DMA((4,)),
        ],
        compiler_params=pltpu.CompilerParams(
            collective_id=0, has_side_effects=True, vmem_limit_bytes=24 << 20
        ),
    )(landmarks, slab_points, panel_points, inverse_blocks)
    return pl.pallas_call(
        finish_kernel,
        name="finish",
        in_specs=[vmem] * 5,
        out_specs=hbm,
        out_shape=jax.ShapeDtypeStruct((8 * CHIP, COLS), F32),
        scratch_shapes=[
            pltpu.VMEM((len(UNITS_B), 2 * HALF, COLS), F32),
            pltpu.SemaphoreType.DMA((32,)),
        ],
        compiler_params=pltpu.CompilerParams(vmem_limit_bytes=24 << 20),
    )(held, res, we, mc, cs)


def solution(mesh):
    in_specs = (P(("row", "col"), None), P("col", None), P(), P())
    return jax.shard_map(
        local, mesh=mesh, in_specs=in_specs, out_specs=P("row", "col"), check_vma=False
    )
```

```python
import functools
import math

import jax
import jax.numpy as jnp
from jax import lax
from jax.experimental import pallas as pl
from jax.experimental.pallas import tpu as pltpu
from jax.sharding import PartitionSpec as P

MESH = pl.DeviceIdType.MESH
F32, BF16 = jnp.float32, jnp.bfloat16
DIM = 128
PANEL = 256
ROWS = 640
PIECE = 128
PARTS = 5
CHIP = 1280
COLS = 256
SCALE = math.log2(math.e) / DIM

UNITS_A = [
    ((0, 0, 0), (0, 1, 0), (0, 2, 0), (0, 3, 0), (0, 4, 0)),
    ((0, 0, 1), (0, 1, 1), (0, 2, 1), (0, 3, 1), (0, 4, 1)),
    ((3, 0, 0), (1, 4, 0), (4, 0, 0), (3, 1, 0), (1, 3, 0)),
    ((4, 1, 0), (3, 0, 1), (1, 4, 1), (4, 0, 1), (3, 1, 1)),
    ((1, 3, 1), (4, 1, 1), (3, 2, 0), (1, 2, 0), (4, 2, 0)),
    ((3, 2, 1), (1, 2, 1), (4, 2, 1), (3, 3, 0), (1, 1, 0)),
    ((4, 3, 0), (3, 3, 1), (1, 1, 1), (4, 3, 1), (3, 4, 0)),
    ((1, 0, 0), (4, 4, 0), (3, 4, 1), (1, 0, 1), (4, 4, 1)),
    ((2, 0, 0), (2, 4, 0), (7, 0, 0), (2, 1, 0), (2, 3, 0)),
    ((2, 0, 1), (2, 4, 1), (7, 0, 1), (2, 1, 1), (2, 3, 1)),
    ((5, 4, 0), (2, 2, 0), (7, 1, 0), (5, 0, 0), (5, 4, 1)),
    ((2, 2, 1), (7, 1, 1), (5, 0, 1), (5, 3, 0), (7, 3, 0)),
    ((5, 1, 0), (5, 3, 1), (7, 3, 1), (5, 1, 1), (7, 2, 0)),
]
UNITS_B = [
    ((7, 2, 1), (5, 2, 0), (5, 2, 1), (7, 4, 0), (7, 4, 1)),
    ((6, 0, 0), (6, 0, 1), (6, 2, 0), (6, 2, 1), (6, 4, 0)),
    ((6, 4, 1), (6, 1, 0), (6, 1, 1), (6, 3, 0), (6, 3, 1)),
]
RUNS = [
    (5, 0, 2, 0), (5, 0, 2, 1), (5, 3, 2, 0), (5, 3, 2, 1), (7, 0, 4, 0), (7, 0, 2, 1), (7, 3, 1, 1),
]
ARRIVALS = {
    1: [
        (3, 0, ((2, "up"), (7, "across"))),
        (1, 4, ((2, "down"), (5, "across"))),
        (4, 0, ()),
    ],
    2: [
        (3, 1, ((2, "up"), (7, "across"))),
        (1, 3, ((2, "down"), (5, "across"))),
        (4, 1, ()),
    ],
    3: [(3, 2, ((2, "up"), (7, "across"))), (1, 2, ()), (4, 2, ())],
    4: [(3, 3, ()), (1, 1, ()), (4, 3, ((7, "up"),))],
    5: [(3, 4, ()), (1, 0, ()), (4, 4, ((7, "up"),))],
    6: [(2, 0, ()), (2, 4, ()), (7, 0, ((6, "up"),))],
    7: [(2, 1, ()), (2, 3, ()), (5, 4, ((6, "down"),))],
    8: [(2, 2, ((6, "across"),)), (7, 1, ((6, "up"),)), (5, 0, ())],
    10: [(5, 3, ((6, "down"),)), (7, 3, ()), (5, 1, ())],
    11: [(7, 2, ()), (7, 4, ()), (5, 2, ())],
    12: [(6, 0, ()), (6, 4, ()), (6, 2, ())],
    13: [(6, 1, ()), (6, 3, ())],
}
LATER = {2: [(4, 0, 5), (4, 1, 5)], 3: [(4, 2, 5)]}


def place():
    me = lax.axis_index("col")
    return me // 4, (me // 2) % 2, me % 2


def dot(a, b):
    return lax.dot_general(a, b, (((1,), (0,)), ((), ())), preferred_element_type=F32)


def dot_full(a, b):
    return lax.dot_general(
        a, b, (((1,), (0,)), ((), ())), precision=lax.Precision.HIGHEST, preferred_element_type=F32
    )


def split(v):
    hi = v.astype(BF16)
    return hi, (v - hi.astype(F32)).astype(BF16)


def offset(piece, core):
    _, part, other = piece
    plane = core if other == 0 else 1 - core
    return pl.multiple_of(plane * ROWS + part * PIECE, PIECE)


def rows_of(held, unit, core):
    return jnp.concatenate([held[p[0], pl.ds(offset(p, core), PIECE), :] for p in unit], axis=0)


def kernel_phase(points, we, cs):
    hi, lo = split(points)
    raw = dot(jnp.concatenate([hi, lo, hi], axis=1), we[...])
    panel = jnp.exp2(raw[:, : 2 * PANEL])
    slab = jnp.exp2(raw[:, 2 * PANEL :] + cs[...])
    scale = jnp.exp2(-SCALE * jnp.sum(points * points, axis=1, keepdims=True))
    ghi, glo = split(panel)
    return jnp.concatenate([ghi, glo, ghi], axis=1), slab, scale


def update_phase(phase, mc):
    panel, slab, scale = phase
    return scale * (slab - dot(panel, mc[...]))


def gather_kernel(
    l_ref, s_ref, p_ref, a_ref, held, res, we, mc, cs, s_v, p_v, a_v, send, recv, loc
):
    z, x, core = place()

    def device(dz, dx, dc):
        return {"col": (((z + dz) % 4) * 2 + (x + dx) % 2) * 2 + (core + dc) % 2}

    partner, across, up, down = device(0, 0, 1), device(0, 1, 0), device(1, 0, 0), device(3, 0, 0)
    ways = {"across": across, "up": up, "down": down}
    barrier = pltpu.get_barrier_semaphore()
    for d in (partner, across, up, down):
        pl.semaphore_signal(barrier, inc=1, device_id=d, device_id_type=MESH)
    own_rows = pl.ds(pl.multiple_of(core * ROWS, ROWS), ROWS)
    local = [
        pltpu.make_async_copy(p_ref, p_v, loc.at[0]),
        pltpu.make_async_copy(s_ref, s_v, loc.at[1]),
        pltpu.make_async_copy(a_ref, a_v, loc.at[2]),
        pltpu.make_async_copy(l_ref, held.at[0, own_rows], loc.at[3]),
    ]
    for copy in local:
        copy.start()
    pl.semaphore_wait(barrier, 4)

    sends = []

    def go(src, slot, part, target):
        copy = pltpu.make_async_remote_copy(
            src_ref=src,
            dst_ref=held.at[slot, pl.ds(offset((slot, part, 0), core), PIECE)],
            send_sem=send.at[len(sends)],
            recv_sem=recv.at[slot, core, part],
            device_id=target,
            device_id_type=MESH,
        )
        copy.start()
        sends.append(copy)

    def mine(slot, part):
        return held.at[slot, pl.ds(offset((slot, part, 0), core), PIECE)]

    def wait(slot, part, other):
        ref = held.at[slot, pl.ds(offset((slot, part, other), core), PIECE)]
        plane = core if other == 0 else 1 - core
        pltpu.make_async_copy(ref, ref, recv.at[slot, plane, part]).wait()

    def before(i):
        for slot, part, onward in ARRIVALS.get(i, ()):
            wait(slot, part, 0)
            go(mine(slot, part), slot, part, partner)
            for there, way in onward:
                go(mine(slot, part), there, part, ways[way])
        for slot, part, there in LATER.get(i, ()):
            go(mine(slot, part), there, part, down)

    def fetch(unit):
        for slot, part, other in unit:
            if other:
                wait(slot, part, 1)

    for i in range(PARTS):
        ahead = l_ref.at[pl.ds(i * PIECE, PIECE)]
        behind = l_ref.at[pl.ds((PARTS - 1 - i) * PIECE, PIECE)]
        go(ahead, 3, i, up)
        go(behind, 1, PARTS - 1 - i, down)
        go(ahead, 4, i, across)
        go(ahead, 0, i, partner)

    local[0].wait()
    local[1].wait()
    panel = p_v[...].reshape(2 * PANEL, DIM)
    turned = jnp.concatenate([panel.T, s_v[...].T], axis=1)
    scaled = turned * (2.0 * SCALE)
    hi, lo = split(scaled)
    we[...] = jnp.concatenate([hi, hi, lo], axis=0)
    columns = -SCALE * jnp.sum(turned * turned, axis=0, keepdims=True)
    cs[...] = columns[:, 2 * PANEL :]
    weights = -SCALE * jnp.sum(panel * panel, axis=1, keepdims=True)
    grid = jnp.exp2(dot_full(panel, scaled[:, 2 * PANEL :]) + weights + columns[:, 2 * PANEL :])
    k0, k1 = grid[:PANEL], grid[PANEL:]
    local[2].wait()
    a0, a1 = a_v[0], a_v[1]
    inv0, inv1 = dot_full(a0.T, a0), dot_full(a1.T, a1)
    g10 = jnp.exp2(dot_full(panel[PANEL:], scaled[:, :PANEL]) + weights[PANEL:] + columns[:, :PANEL])
    qt = dot_full(g10, inv0)
    m1 = dot_full(inv1, k1 - dot_full(qt, k0))
    m0 = dot_full(inv0, k0) - dot_full(qt.T, m1)
    scale_rows = jnp.exp2(weights)
    mhi, mlo = split(jnp.concatenate([m0, m1], axis=0) * scale_rows)
    mc[...] = jnp.concatenate([mhi, mhi, mlo], axis=0)
    local[3].wait()

    pending = []

    def begin(unit):
        pending.append((unit, kernel_phase(rows_of(held, unit, core), we, cs)))

    def finish():
        unit, phase = pending.pop(0)
        out = update_phase(phase, mc)
        for n, piece in enumerate(unit):
            res[piece[0], pl.ds(offset(piece, core), PIECE), :] = out[n * PIECE : (n + 1) * PIECE]

    for i, unit in enumerate(UNITS_A):
        before(i)
        fetch(unit)
        begin(unit)
        if i:
            finish()
    finish()
    before(len(UNITS_A))
    for unit in UNITS_B:
        fetch(unit)
    for copy in sends:
        copy.wait_send()


def finish_kernel(held, res, we, mc, cs, out, last, sems):
    z, x, core = place()
    copies = []

    def put(src, slot, start, size):
        chip = ((z + slot % 4) % 4) * 2 + (x + slot // 4) % 2
        target = out.at[pl.ds(pl.multiple_of(chip * CHIP + start, PIECE), size)]
        copy = pltpu.make_async_copy(src, target, sems.at[len(copies)])
        copy.start()
        copies.append(copy)

    for slot in (0, 4, 3, 1, 2):
        put(res.at[slot], slot, 0, CHIP)
    for slot, part, parts, other in RUNS:
        start = offset((slot, part, other), core)
        put(res.at[slot, pl.ds(start, parts * PIECE)], slot, start, parts * PIECE)
    for n, unit in enumerate(UNITS_B):
        phase = kernel_phase(rows_of(held, unit, core), we, cs)
        last[n] = update_phase(phase, mc)
        for m, piece in enumerate(unit):
            put(last.at[n, pl.ds(m * PIECE, PIECE)], piece[0], offset(piece, core), PIECE)
    for copy in copies:
        copy.wait()


def local(landmarks, slab_points, panel_points, inverse_blocks):
    hbm = pl.BlockSpec(memory_space=pltpu.HBM)
    vmem = pl.BlockSpec(memory_space=pltpu.VMEM)
    arguments = [
        pltpu.with_memory_space_constraint(v, pltpu.HBM)
        for v in (landmarks, slab_points, panel_points, inverse_blocks)
    ]
    held, res, we, mc, cs = pl.pallas_call(
        gather_kernel,
        name="gather",
        in_specs=[hbm] * 4,
        out_specs=[vmem] * 5,
        out_shape=[
            pltpu.VMEM((8, CHIP, DIM), F32),
            pltpu.VMEM((8, CHIP, COLS), F32),
            pltpu.VMEM((3 * DIM, 2 * PANEL + COLS), BF16),
            pltpu.VMEM((6 * PANEL, COLS), BF16),
            pltpu.VMEM((1, COLS), F32),
        ],
        scratch_shapes=[
            pltpu.VMEM((COLS, DIM), F32),
            pltpu.VMEM((2, PANEL, DIM), F32),
            pltpu.VMEM((2, PANEL, PANEL), F32),
            pltpu.SemaphoreType.DMA((96,)),
            pltpu.SemaphoreType.DMA((8, 2, PARTS)),
            pltpu.SemaphoreType.DMA((4,)),
        ],
        compiler_params=pltpu.CompilerParams(
            collective_id=0, has_side_effects=True, vmem_limit_bytes=24 << 20
        ),
    )(*arguments)
    return pl.pallas_call(
        finish_kernel,
        name="finish",
        in_specs=[vmem] * 5,
        out_specs=hbm,
        out_shape=jax.ShapeDtypeStruct((8 * CHIP, COLS), F32),
        scratch_shapes=[
            pltpu.VMEM((len(UNITS_B), ROWS, COLS), F32),
            pltpu.SemaphoreType.DMA((32,)),
        ],
        compiler_params=pltpu.CompilerParams(vmem_limit_bytes=24 << 20),
    )(held, res, we, mc, cs)


def solution(mesh):
    in_specs = (P(("row", "col"), None), P("col", None), P(), P())
    return jax.shard_map(
        local, mesh=mesh, in_specs=in_specs, out_specs=P("row", "col"), check_vma=False
    )
```

```python
import functools
import math

import jax
import jax.numpy as jnp
from jax import lax
from jax.experimental import pallas as pl
from jax.experimental.pallas import tpu as pltpu
from jax.sharding import PartitionSpec as P

MESH = pl.DeviceIdType.MESH
F32, BF16 = jnp.float32, jnp.bfloat16
DIM = 128
PANEL = 256
ROWS = 640
PIECE = 128
PARTS = 5
CHIP = 1280
COLS = 256
SCALE = math.log2(math.e) / DIM

UNITS_A = [
    ((0, 0, 0), (0, 1, 0), (0, 2, 0), (0, 3, 0), (0, 4, 0)),
    ((0, 0, 1), (0, 1, 1), (0, 2, 1), (0, 3, 1), (0, 4, 1)),
    ((3, 0, 0), (1, 4, 0), (4, 0, 0), (3, 1, 0), (1, 3, 0)),
    ((4, 1, 0), (3, 0, 1), (1, 4, 1), (4, 0, 1), (3, 2, 0)),
    ((1, 2, 0), (4, 2, 0), (3, 1, 1), (1, 3, 1), (4, 1, 1)),
    ((3, 3, 0), (1, 1, 0), (4, 3, 0), (3, 2, 1), (1, 2, 1)),
    ((3, 4, 0), (1, 0, 0), (4, 4, 0), (4, 2, 1), (3, 3, 1)),
    ((2, 0, 0), (2, 4, 0), (7, 0, 0), (1, 1, 1), (4, 3, 1)),
    ((2, 1, 0), (2, 3, 0), (5, 4, 0), (3, 4, 1), (1, 0, 1)),
    ((2, 2, 0), (7, 1, 0), (5, 0, 0), (4, 4, 1), (2, 0, 1)),
    ((5, 3, 0), (7, 3, 0), (5, 1, 0), (2, 4, 1), (7, 0, 1)),
    ((2, 1, 1), (2, 3, 1), (5, 4, 1), (2, 2, 1), (7, 1, 1)),
    ((7, 4, 0), (5, 2, 0), (7, 2, 0), (5, 0, 1), (5, 3, 1)),
]
UNITS_B = [
    ((5, 1, 1), (7, 3, 1), (7, 2, 1), (5, 2, 1), (7, 4, 1)),
    ((6, 0, 0), (6, 0, 1), (6, 2, 0), (6, 2, 1), (6, 4, 0)),
    ((6, 4, 1), (6, 1, 0), (6, 1, 1), (6, 3, 0), (6, 3, 1)),
]
DONE = (0, 4, 3, 1, 2)
RUNS = [
    (5, 0, 5, 0),
    (5, 0, 1, 1),
    (5, 3, 2, 1),
    (7, 0, 5, 0),
    (7, 0, 2, 1),
]
ARRIVALS = {
    1: [
        (3, 0, ((2, 'up'), (7, 'across'))),
        (1, 4, ((2, 'down'), (5, 'across'))),
        (4, 0, ()),
    ],
    2: [
        (3, 1, ((2, 'up'), (7, 'across'))),
        (1, 3, ((2, 'down'), (5, 'across'))),
        (4, 1, ()),
    ],
    3: [
        (3, 2, ((2, 'up'), (7, 'across'))),
        (1, 2, ()),
        (4, 2, ()),
    ],
    4: [
        (3, 3, ()),
        (1, 1, ()),
        (4, 3, ((7, 'up'),)),
    ],
    6: [
        (3, 4, ()),
        (1, 0, ()),
        (4, 4, ((7, 'up'),)),
    ],
    7: [
        (2, 0, ()),
        (2, 4, ()),
        (7, 0, ((6, 'up'),)),
    ],
    8: [
        (2, 1, ()),
        (2, 3, ()),
        (5, 4, ((6, 'down'),)),
    ],
    9: [
        (2, 2, ((6, 'across'),)),
        (7, 1, ((6, 'up'),)),
        (5, 0, ()),
    ],
    10: [
        (5, 3, ((6, 'down'),)),
        (7, 3, ()),
        (5, 1, ()),
    ],
    12: [
        (7, 4, ()),
        (5, 2, ()),
        (7, 2, ()),
        (6, 0, ()),
        (6, 4, ()),
        (6, 2, ()),
    ],
    13: [
        (6, 1, ()),
        (6, 3, ()),
    ],
}
LATER = {2: [(4, 0, 5), (4, 1, 5)], 3: [(4, 2, 5)]}


def place():
    me = lax.axis_index("col")
    return me // 4, (me // 2) % 2, me % 2


def dot(a, b):
    return lax.dot_general(a, b, (((1,), (0,)), ((), ())), preferred_element_type=F32)


def split(v):
    hi = v.astype(BF16)
    return hi, (v - hi.astype(F32)).astype(BF16)


def dot_full(a, b):
    return lax.dot_general(
        a, b, (((1,), (0,)), ((), ())), precision=lax.Precision.HIGHEST, preferred_element_type=F32
    )


def offset(piece, core):
    _, part, other = piece
    plane = core if other == 0 else 1 - core
    return pl.multiple_of(plane * ROWS + part * PIECE, PIECE)


def rows_of(held, unit, core):
    return jnp.concatenate([held[p[0], pl.ds(offset(p, core), PIECE), :] for p in unit], axis=0)


def kernel_phase(points, we, cs):
    hi, lo = split(points)
    raw = dot(jnp.concatenate([hi, lo, hi], axis=1), we[...])
    panel = jnp.exp2(raw[:, : 2 * PANEL])
    slab = jnp.exp2(raw[:, 2 * PANEL :] + cs[...])
    scale = jnp.exp2(-SCALE * jnp.sum(points * points, axis=1, keepdims=True))
    ghi, glo = split(panel)
    return jnp.concatenate([ghi, glo, ghi], axis=1), slab, scale


def update_phase(phase, mc):
    panel, slab, scale = phase
    return scale * (slab - dot(panel, mc[...]))


def gather_kernel(
    l_ref, s_ref, p_ref, a_ref, held, res, we, mc, cs, s_v, p_v, a_v, send, recv, loc
):
    z, x, core = place()

    def device(dz, dx, dc):
        return {"col": (((z + dz) % 4) * 2 + (x + dx) % 2) * 2 + (core + dc) % 2}

    partner, across, up, down = device(0, 0, 1), device(0, 1, 0), device(1, 0, 0), device(3, 0, 0)
    ways = {"across": across, "up": up, "down": down}
    barrier = pltpu.get_barrier_semaphore()
    for d in (partner, across, up, down):
        pl.semaphore_signal(barrier, inc=1, device_id=d, device_id_type=MESH)
    own_rows = pl.ds(pl.multiple_of(core * ROWS, ROWS), ROWS)
    local = [
        pltpu.make_async_copy(p_ref, p_v, loc.at[0]),
        pltpu.make_async_copy(s_ref, s_v, loc.at[1]),
        pltpu.make_async_copy(a_ref, a_v, loc.at[2]),
        pltpu.make_async_copy(l_ref, held.at[0, own_rows], loc.at[3]),
    ]
    for copy in local:
        copy.start()
    pl.semaphore_wait(barrier, 4)

    sends = []

    def go(src, slot, part, target):
        copy = pltpu.make_async_remote_copy(
            src_ref=src,
            dst_ref=held.at[slot, pl.ds(offset((slot, part, 0), core), PIECE)],
            send_sem=send.at[len(sends)],
            recv_sem=recv.at[slot, core, part],
            device_id=target,
            device_id_type=MESH,
        )
        copy.start()
        sends.append(copy)

    def mine(slot, part):
        return held.at[slot, pl.ds(offset((slot, part, 0), core), PIECE)]

    def wait(slot, part, other):
        ref = held.at[slot, pl.ds(offset((slot, part, other), core), PIECE)]
        plane = core if other == 0 else 1 - core
        pltpu.make_async_copy(ref, ref, recv.at[slot, plane, part]).wait()

    def before(i):
        for slot, part, onward in ARRIVALS.get(i, ()):
            wait(slot, part, 0)
            go(mine(slot, part), slot, part, partner)
            for there, way in onward:
                go(mine(slot, part), there, part, ways[way])
        for slot, part, there in LATER.get(i, ()):
            go(mine(slot, part), there, part, down)

    def fetch(unit):
        for slot, part, other in unit:
            if other:
                wait(slot, part, 1)

    for i in range(PARTS):
        ahead = l_ref.at[pl.ds(i * PIECE, PIECE)]
        behind = l_ref.at[pl.ds((PARTS - 1 - i) * PIECE, PIECE)]
        go(ahead, 3, i, up)
        go(behind, 1, PARTS - 1 - i, down)
        go(ahead, 4, i, across)
        go(ahead, 0, i, partner)

    local[0].wait()
    local[1].wait()
    panel = p_v[...].reshape(2 * PANEL, DIM)
    turned = jnp.concatenate([panel.T, s_v[...].T], axis=1)
    scaled = turned * (2.0 * SCALE)
    hi, lo = split(scaled)
    we[...] = jnp.concatenate([hi, hi, lo], axis=0)
    columns = -SCALE * jnp.sum(turned * turned, axis=0, keepdims=True)
    cs[...] = columns[:, 2 * PANEL :]
    weights = -SCALE * jnp.sum(panel * panel, axis=1, keepdims=True)
    grid = jnp.exp2(dot_full(panel, scaled[:, 2 * PANEL :]) + weights + columns[:, 2 * PANEL :])
    k0, k1 = grid[:PANEL], grid[PANEL:]
    local[2].wait()
    a0, a1 = a_v[0], a_v[1]
    inv0, inv1 = dot_full(a0.T, a0), dot_full(a1.T, a1)
    g10 = jnp.exp2(dot_full(panel[PANEL:], scaled[:, :PANEL]) + weights[PANEL:] + columns[:, :PANEL])
    qt = dot_full(g10, inv0)
    m1 = dot_full(inv1, k1 - dot_full(qt, k0))
    m0 = dot_full(inv0, k0) - dot_full(qt.T, m1)
    scale_rows = jnp.exp2(weights)
    mhi, mlo = split(jnp.concatenate([m0, m1], axis=0) * scale_rows)
    mc[...] = jnp.concatenate([mhi, mhi, mlo], axis=0)
    local[3].wait()

    pending = []

    def begin(unit):
        pending.append((unit, kernel_phase(rows_of(held, unit, core), we, cs)))

    def finish():
        unit, phase = pending.pop(0)
        out = update_phase(phase, mc)
        for n, piece in enumerate(unit):
            res[piece[0], pl.ds(offset(piece, core), PIECE), :] = out[n * PIECE : (n + 1) * PIECE]

    for i, unit in enumerate(UNITS_A):
        before(i)
        if unit is UNITS_A[-1]:
            before(i + 1)
        fetch(unit)
        begin(unit)
        if i:
            finish()
    finish()
    for unit in UNITS_B:
        fetch(unit)
    for copy in sends:
        copy.wait_send()


def finish_kernel(held, res, we, mc, cs, out, last, sems):
    z, x, core = place()
    copies = []

    def put(src, slot, start, size):
        chip = ((z + slot % 4) % 4) * 2 + (x + slot // 4) % 2
        target = out.at[pl.ds(pl.multiple_of(chip * CHIP + start, PIECE), size)]
        copy = pltpu.make_async_copy(src, target, sems.at[len(copies)])
        copy.start()
        copies.append(copy)

    for slot in DONE:
        put(res.at[slot], slot, 0, CHIP)
    for slot, part, parts, other in RUNS:
        start = offset((slot, part, other), core)
        put(res.at[slot, pl.ds(start, parts * PIECE)], slot, start, parts * PIECE)
    for n, unit in enumerate(UNITS_B):
        phase = kernel_phase(rows_of(held, unit, core), we, cs)
        last[n] = update_phase(phase, mc)
        for m, piece in enumerate(unit):
            put(last.at[n, pl.ds(m * PIECE, PIECE)], piece[0], offset(piece, core), PIECE)
    for copy in copies:
        copy.wait()


def local(landmarks, slab_points, panel_points, inverse_blocks):
    hbm = pl.BlockSpec(memory_space=pltpu.HBM)
    vmem = pl.BlockSpec(memory_space=pltpu.VMEM)
    arguments = [
        pltpu.with_memory_space_constraint(v, pltpu.HBM)
        for v in (landmarks, slab_points, panel_points, inverse_blocks)
    ]
    held, res, we, mc, cs = pl.pallas_call(
        gather_kernel,
        name="gather",
        in_specs=[hbm] * 4,
        out_specs=[vmem] * 5,
        out_shape=[
            pltpu.VMEM((8, CHIP, DIM), F32),
            pltpu.VMEM((8, CHIP, COLS), F32),
            pltpu.VMEM((3 * DIM, 2 * PANEL + COLS), BF16),
            pltpu.VMEM((6 * PANEL, COLS), BF16),
            pltpu.VMEM((1, COLS), F32),
        ],
        scratch_shapes=[
            pltpu.VMEM((COLS, DIM), F32),
            pltpu.VMEM((2, PANEL, DIM), F32),
            pltpu.VMEM((2, PANEL, PANEL), F32),
            pltpu.SemaphoreType.DMA((96,)),
            pltpu.SemaphoreType.DMA((8, 2, PARTS)),
            pltpu.SemaphoreType.DMA((4,)),
        ],
        compiler_params=pltpu.CompilerParams(
            collective_id=0, has_side_effects=True, vmem_limit_bytes=24 << 20
        ),
    )(*arguments)
    return pl.pallas_call(
        finish_kernel,
        name="finish",
        in_specs=[vmem] * 5,
        out_specs=hbm,
        out_shape=jax.ShapeDtypeStruct((8 * CHIP, COLS), F32),
        scratch_shapes=[
            pltpu.VMEM((len(UNITS_B), ROWS, COLS), F32),
            pltpu.SemaphoreType.DMA((32,)),
        ],
        compiler_params=pltpu.CompilerParams(vmem_limit_bytes=24 << 20),
    )(held, res, we, mc, cs)


def solution(mesh):
    in_specs = (P(("row", "col"), None), P("col", None), P(), P())
    return jax.shard_map(
        local, mesh=mesh, in_specs=in_specs, out_specs=P("row", "col"), check_vma=False
    )
```

```python
import functools
import math

import jax
import jax.numpy as jnp
from jax import lax
from jax.experimental import pallas as pl
from jax.experimental.pallas import tpu as pltpu
from jax.sharding import PartitionSpec as P

MESH = pl.DeviceIdType.MESH
F32, BF16 = jnp.float32, jnp.bfloat16
DIM = 128
PANEL = 256
ROWS = 640
PIECE = 128
PARTS = 5
CHIP = 1280
COLS = 256
SCALE = math.log2(math.e) / DIM

UNITS_A = [
    ((0, 0, 0), (0, 1, 0), (0, 2, 0), (0, 3, 0), (0, 4, 0)),
    ((0, 0, 1), (0, 1, 1), (0, 2, 1), (0, 3, 1), (0, 4, 1)),
    ((3, 0, 0), (1, 4, 0), (4, 0, 0), (3, 1, 0), (1, 3, 0)),
    ((4, 1, 0), (3, 0, 1), (1, 4, 1), (4, 0, 1), (3, 2, 0)),
    ((1, 2, 0), (4, 2, 0), (3, 1, 1), (1, 3, 1), (4, 1, 1)),
    ((3, 3, 0), (1, 1, 0), (4, 3, 0), (3, 2, 1), (1, 2, 1)),
    ((3, 4, 0), (1, 0, 0), (4, 4, 0), (4, 2, 1), (3, 3, 1)),
    ((2, 0, 0), (2, 4, 0), (7, 0, 0), (1, 1, 1), (4, 3, 1)),
    ((2, 1, 0), (2, 3, 0), (5, 4, 0), (3, 4, 1), (1, 0, 1)),
    ((2, 2, 0), (7, 1, 0), (5, 0, 0), (4, 4, 1), (2, 0, 1)),
    ((5, 3, 0), (7, 3, 0), (5, 1, 0), (2, 4, 1), (7, 0, 1)),
    ((2, 1, 1), (2, 3, 1), (5, 4, 1), (2, 2, 1), (7, 1, 1)),
    ((7, 4, 0), (5, 2, 0), (7, 2, 0), (5, 0, 1), (5, 3, 1)),
]
UNITS_B = [
    ((5, 1, 1), (7, 3, 1), (7, 2, 1), (5, 2, 1), (7, 4, 1)),
    ((6, 0, 0), (6, 0, 1), (6, 2, 0), (6, 2, 1), (6, 4, 0)),
    ((6, 4, 1), (6, 1, 0), (6, 1, 1), (6, 3, 0), (6, 3, 1)),
]
DONE = (0, 4, 3, 1, 2)
RUNS = [
    (5, 0, 5, 0),
    (5, 0, 1, 1),
    (5, 3, 2, 1),
    (7, 0, 5, 0),
    (7, 0, 2, 1),
]
ARRIVALS = {
    1: [
        (3, 0, ((2, 'up'), (7, 'across'))),
        (1, 4, ((2, 'down'), (5, 'across'))),
        (4, 0, ()),
    ],
    2: [
        (3, 1, ((2, 'up'), (7, 'across'))),
        (1, 3, ((2, 'down'), (5, 'across'))),
        (4, 1, ()),
    ],
    3: [
        (3, 2, ((2, 'up'), (7, 'across'))),
        (1, 2, ()),
        (4, 2, ()),
    ],
    4: [
        (3, 3, ()),
        (1, 1, ()),
        (4, 3, ((7, 'up'),)),
    ],
    6: [
        (3, 4, ()),
        (1, 0, ()),
        (4, 4, ((7, 'up'),)),
    ],
    7: [
        (2, 0, ()),
        (2, 4, ()),
        (7, 0, ((6, 'up'),)),
    ],
    8: [
        (2, 1, ()),
        (2, 3, ()),
        (5, 4, ((6, 'down'),)),
    ],
    9: [
        (2, 2, ((6, 'across'),)),
        (7, 1, ((6, 'up'),)),
        (5, 0, ()),
    ],
    10: [
        (5, 3, ((6, 'down'),)),
        (7, 3, ()),
        (5, 1, ()),
    ],
    11: [
        (7, 4, ()),
        (5, 2, ()),
        (7, 2, ()),
    ],
    12: [
        (6, 0, ()),
        (6, 4, ()),
        (6, 2, ()),
    ],
    13: [
        (6, 1, ()),
        (6, 3, ()),
    ],
}
LATER = {2: [(4, 0, 5), (4, 1, 5)], 3: [(4, 2, 5)]}


def place():
    me = lax.axis_index("col")
    return me // 4, (me // 2) % 2, me % 2


def dot(a, b):
    return lax.dot_general(a, b, (((1,), (0,)), ((), ())), preferred_element_type=F32)


def split(v):
    hi = v.astype(BF16)
    return hi, (v - hi.astype(F32)).astype(BF16)


def dot_full(a, b):
    return lax.dot_general(
        a, b, (((1,), (0,)), ((), ())), precision=lax.Precision.HIGHEST, preferred_element_type=F32
    )


def offset(piece, core):
    _, part, other = piece
    plane = core if other == 0 else 1 - core
    return pl.multiple_of(plane * ROWS + part * PIECE, PIECE)


def rows_of(held, unit, core):
    return jnp.concatenate([held[p[0], pl.ds(offset(p, core), PIECE), :] for p in unit], axis=0)


def kernel_phase(points, we, cs):
    hi, lo = split(points)
    raw = dot(jnp.concatenate([hi, lo, hi], axis=1), we[...])
    panel = jnp.exp2(raw[:, : 2 * PANEL])
    slab = jnp.exp2(raw[:, 2 * PANEL :] + cs[...])
    scale = jnp.exp2(-SCALE * jnp.sum(points * points, axis=1, keepdims=True))
    ghi, glo = split(panel)
    return jnp.concatenate([ghi, glo, ghi], axis=1), slab, scale


def update_phase(phase, mc):
    panel, slab, scale = phase
    return scale * (slab - dot(panel, mc[...]))


def gather_kernel(
    l_ref, s_ref, p_ref, a_ref, held, res, we, mc, cs, s_v, p_v, a_v, send, recv, loc
):
    z, x, core = place()

    def device(dz, dx, dc):
        return {"col": (((z + dz) % 4) * 2 + (x + dx) % 2) * 2 + (core + dc) % 2}

    partner, across, up, down = device(0, 0, 1), device(0, 1, 0), device(1, 0, 0), device(3, 0, 0)
    ways = {"across": across, "up": up, "down": down}
    barrier = pltpu.get_barrier_semaphore()
    for d in (partner, across, up, down):
        pl.semaphore_signal(barrier, inc=1, device_id=d, device_id_type=MESH)
    own_rows = pl.ds(pl.multiple_of(core * ROWS, ROWS), ROWS)
    local = [
        pltpu.make_async_copy(p_ref, p_v, loc.at[0]),
        pltpu.make_async_copy(s_ref, s_v, loc.at[1]),
        pltpu.make_async_copy(a_ref, a_v, loc.at[2]),
        pltpu.make_async_copy(l_ref, held.at[0, own_rows], loc.at[3]),
    ]
    for n in (0, 1, 3, 2):
        local[n].start()
    pl.semaphore_wait(barrier, 4)

    sends = []

    def go(src, slot, part, target):
        copy = pltpu.make_async_remote_copy(
            src_ref=src,
            dst_ref=held.at[slot, pl.ds(offset((slot, part, 0), core), PIECE)],
            send_sem=send.at[len(sends)],
            recv_sem=recv.at[slot, core, part],
            device_id=target,
            device_id_type=MESH,
        )
        copy.start()
        sends.append(copy)

    def mine(slot, part):
        return held.at[slot, pl.ds(offset((slot, part, 0), core), PIECE)]

    def wait(slot, part, other):
        ref = held.at[slot, pl.ds(offset((slot, part, other), core), PIECE)]
        plane = core if other == 0 else 1 - core
        pltpu.make_async_copy(ref, ref, recv.at[slot, plane, part]).wait()

    def before(i):
        for slot, part, onward in ARRIVALS.get(i, ()):
            wait(slot, part, 0)
            go(mine(slot, part), slot, part, partner)
            for there, way in onward:
                go(mine(slot, part), there, part, ways[way])
        for slot, part, there in LATER.get(i, ()):
            go(mine(slot, part), there, part, down)

    def fetch(unit):
        for slot, part, other in unit:
            if other:
                wait(slot, part, 1)

    for i in range(PARTS):
        ahead = l_ref.at[pl.ds(i * PIECE, PIECE)]
        behind = l_ref.at[pl.ds((PARTS - 1 - i) * PIECE, PIECE)]
        go(ahead, 3, i, up)
        go(behind, 1, PARTS - 1 - i, down)
        go(ahead, 4, i, across)
        go(ahead, 0, i, partner)

    local[0].wait()
    local[1].wait()
    panel = p_v[...].reshape(2 * PANEL, DIM)
    turned = jnp.concatenate([panel.T, s_v[...].T], axis=1)
    scaled = turned * (2.0 * SCALE)
    hi, lo = split(scaled)
    we[...] = jnp.concatenate([hi, hi, lo], axis=0)
    columns = -SCALE * jnp.sum(turned * turned, axis=0, keepdims=True)
    cs[...] = columns[:, 2 * PANEL :]
    local[3].wait()
    pending = []

    def begin(unit):
        pending.append((unit, kernel_phase(rows_of(held, unit, core), we, cs)))

    begin(UNITS_A[0])
    weights = -SCALE * jnp.sum(panel * panel, axis=1, keepdims=True)
    grid = jnp.exp2(dot_full(panel, scaled[:, 2 * PANEL :]) + weights + columns[:, 2 * PANEL :])
    k0, k1 = grid[:PANEL], grid[PANEL:]
    local[2].wait()
    a0, a1 = a_v[0], a_v[1]
    inv0, inv1 = dot_full(a0.T, a0), dot_full(a1.T, a1)
    g10 = jnp.exp2(dot_full(panel[PANEL:], scaled[:, :PANEL]) + weights[PANEL:] + columns[:, :PANEL])
    qt = dot_full(g10, inv0)
    m1 = dot_full(inv1, k1 - dot_full(qt, k0))
    m0 = dot_full(inv0, k0) - dot_full(qt.T, m1)
    scale_rows = jnp.exp2(weights)
    mhi, mlo = split(jnp.concatenate([m0, m1], axis=0) * scale_rows)
    mc[...] = jnp.concatenate([mhi, mhi, mlo], axis=0)
    def finish():
        unit, phase = pending.pop(0)
        out = update_phase(phase, mc)
        for n, piece in enumerate(unit):
            res[piece[0], pl.ds(offset(piece, core), PIECE), :] = out[n * PIECE : (n + 1) * PIECE]

    for i, unit in enumerate(UNITS_A):
        before(i)
        if unit is UNITS_A[-1]:
            before(i + 1)
        fetch(unit)
        if i:
            begin(unit)
            finish()
    finish()
    for unit in UNITS_B:
        fetch(unit)
    for copy in sends:
        copy.wait_send()


def finish_kernel(held, res, we, mc, cs, out, last, sems):
    z, x, core = place()
    copies = []

    def put(src, slot, start, size):
        chip = ((z + slot % 4) % 4) * 2 + (x + slot // 4) % 2
        target = out.at[pl.ds(pl.multiple_of(chip * CHIP + start, PIECE), size)]
        copy = pltpu.make_async_copy(src, target, sems.at[len(copies)])
        copy.start()
        copies.append(copy)

    for slot in DONE:
        put(res.at[slot], slot, 0, CHIP)
    for slot, part, parts, other in RUNS:
        start = offset((slot, part, other), core)
        put(res.at[slot, pl.ds(start, parts * PIECE)], slot, start, parts * PIECE)
    for n, unit in enumerate(UNITS_B):
        phase = kernel_phase(rows_of(held, unit, core), we, cs)
        last[n] = update_phase(phase, mc)
        for m, piece in enumerate(unit):
            put(last.at[n, pl.ds(m * PIECE, PIECE)], piece[0], offset(piece, core), PIECE)
    for copy in copies:
        copy.wait()


def local(landmarks, slab_points, panel_points, inverse_blocks):
    hbm = pl.BlockSpec(memory_space=pltpu.HBM)
    vmem = pl.BlockSpec(memory_space=pltpu.VMEM)
    arguments = [
        pltpu.with_memory_space_constraint(v, pltpu.HBM)
        for v in (landmarks, slab_points, panel_points, inverse_blocks)
    ]
    held, res, we, mc, cs = pl.pallas_call(
        gather_kernel,
        name="gather",
        in_specs=[hbm] * 4,
        out_specs=[vmem] * 5,
        out_shape=[
            pltpu.VMEM((8, CHIP, DIM), F32),
            pltpu.VMEM((8, CHIP, COLS), F32),
            pltpu.VMEM((3 * DIM, 2 * PANEL + COLS), BF16),
            pltpu.VMEM((6 * PANEL, COLS), BF16),
            pltpu.VMEM((1, COLS), F32),
        ],
        scratch_shapes=[
            pltpu.VMEM((COLS, DIM), F32),
            pltpu.VMEM((2, PANEL, DIM), F32),
            pltpu.VMEM((2, PANEL, PANEL), F32),
            pltpu.SemaphoreType.DMA((96,)),
            pltpu.SemaphoreType.DMA((8, 2, PARTS)),
            pltpu.SemaphoreType.DMA((4,)),
        ],
        compiler_params=pltpu.CompilerParams(
            collective_id=0, has_side_effects=True, vmem_limit_bytes=24 << 20
        ),
    )(*arguments)
    return pl.pallas_call(
        finish_kernel,
        name="finish",
        in_specs=[vmem] * 5,
        out_specs=hbm,
        out_shape=jax.ShapeDtypeStruct((8 * CHIP, COLS), F32),
        scratch_shapes=[
            pltpu.VMEM((len(UNITS_B), ROWS, COLS), F32),
            pltpu.SemaphoreType.DMA((32,)),
        ],
        compiler_params=pltpu.CompilerParams(vmem_limit_bytes=24 << 20),
    )(held, res, we, mc, cs)


def solution(mesh):
    in_specs = (P(("row", "col"), None), P("col", None), P(), P())
    return jax.shard_map(
        local, mesh=mesh, in_specs=in_specs, out_specs=P("row", "col"), check_vma=False
    )
```

```python
import functools
import math

import jax
import jax.numpy as jnp
from jax import lax
from jax.experimental import pallas as pl
from jax.experimental.pallas import tpu as pltpu
from jax.sharding import PartitionSpec as P

MESH = pl.DeviceIdType.MESH
F32, BF16 = jnp.float32, jnp.bfloat16
DIM = 128
PANEL = 256
ROWS = 640
PIECE = 128
PARTS = 5
CHIP = 1280
COLS = 256
SCALE = math.log2(math.e) / DIM

UNITS_A = [
    ((0, 0, 0), (0, 1, 0), (0, 2, 0), (0, 3, 0), (0, 4, 0)),
    ((0, 0, 1), (0, 1, 1), (0, 2, 1), (0, 3, 1), (0, 4, 1)),
    ((3, 0, 0), (1, 4, 0), (4, 0, 0), (3, 1, 0), (1, 3, 0)),
    ((4, 1, 0), (3, 0, 1), (1, 4, 1), (4, 0, 1), (3, 2, 0)),
    ((1, 2, 0), (4, 2, 0), (3, 1, 1), (1, 3, 1), (4, 1, 1)),
    ((3, 3, 0), (1, 1, 0), (4, 3, 0), (3, 2, 1), (1, 2, 1)),
    ((3, 4, 0), (1, 0, 0), (4, 4, 0), (4, 2, 1), (3, 3, 1)),
    ((2, 0, 0), (2, 4, 0), (7, 0, 0), (1, 1, 1), (4, 3, 1)),
    ((2, 1, 0), (2, 3, 0), (5, 4, 0), (3, 4, 1), (1, 0, 1)),
    ((2, 2, 0), (7, 1, 0), (5, 0, 0), (4, 4, 1), (2, 0, 1)),
    ((5, 3, 0), (7, 3, 0), (5, 1, 0), (2, 4, 1), (7, 0, 1)),
    ((2, 1, 1), (2, 3, 1), (5, 4, 1), (2, 2, 1), (7, 1, 1)),
    ((7, 4, 0), (5, 2, 0), (7, 2, 0), (5, 0, 1), (5, 3, 1)),
]
UNITS_B = [
    ((5, 1, 1), (7, 3, 1), (7, 2, 1), (5, 2, 1), (7, 4, 1)),
    ((6, 0, 0), (6, 0, 1), (6, 2, 0), (6, 2, 1), (6, 4, 0)),
    ((6, 4, 1), (6, 1, 0), (6, 1, 1), (6, 3, 0), (6, 3, 1)),
]
DONE = (0, 4, 3, 1, 2)
RUNS = [
    (5, 0, 5, 0),
    (5, 0, 1, 1),
    (5, 3, 2, 1),
    (7, 0, 5, 0),
    (7, 0, 2, 1),
]
ARRIVALS = {
    1: [
        (3, 0, ((2, 'up'), (7, 'across'))),
        (1, 4, ((2, 'down'), (5, 'across'))),
        (4, 0, ()),
    ],
    2: [
        (3, 1, ((2, 'up'), (7, 'across'))),
        (1, 3, ((2, 'down'), (5, 'across'))),
        (4, 1, ()),
    ],
    3: [
        (3, 2, ((2, 'up'), (7, 'across'))),
        (1, 2, ()),
        (4, 2, ()),
    ],
    4: [
        (3, 3, ()),
        (1, 1, ()),
        (4, 3, ((7, 'up'),)),
    ],
    6: [
        (3, 4, ()),
        (1, 0, ()),
        (4, 4, ((7, 'up'),)),
    ],
    7: [
        (2, 0, ()),
        (2, 4, ()),
        (7, 0, ((6, 'up'),)),
    ],
    8: [
        (2, 1, ()),
        (2, 3, ()),
        (5, 4, ((6, 'down'),)),
    ],
    9: [
        (2, 2, ((6, 'across'),)),
        (7, 1, ((6, 'up'),)),
        (5, 0, ()),
    ],
    10: [
        (5, 3, ((6, 'down'),)),
        (7, 3, ()),
        (5, 1, ()),
    ],
    11: [
        (7, 4, ()),
        (5, 2, ()),
        (7, 2, ()),
    ],
    12: [
        (6, 0, ()),
        (6, 4, ()),
        (6, 2, ()),
    ],
    13: [
        (6, 1, ()),
        (6, 3, ()),
    ],
}
LATER = {2: [(4, 0, 5), (4, 1, 5)], 3: [(4, 2, 5)]}


def place():
    me = lax.axis_index("col")
    return me // 4, (me // 2) % 2, me % 2


def dot(a, b):
    return lax.dot_general(a, b, (((1,), (0,)), ((), ())), preferred_element_type=F32)


def split(v):
    hi = v.astype(BF16)
    return hi, (v - hi.astype(F32)).astype(BF16)


def dot_full(a, b):
    return lax.dot_general(
        a, b, (((1,), (0,)), ((), ())), precision=lax.Precision.HIGHEST, preferred_element_type=F32
    )


def offset(piece, core):
    _, part, other = piece
    plane = core if other == 0 else 1 - core
    return pl.multiple_of(plane * ROWS + part * PIECE, PIECE)


def rows_of(held, unit, core):
    return jnp.concatenate([held[p[0], pl.ds(offset(p, core), PIECE), :] for p in unit], axis=0)


def kernel_phase(points, we, cs):
    hi, lo = split(points)
    raw = dot(jnp.concatenate([hi, lo, hi], axis=1), we[...])
    panel = jnp.exp2(raw[:, : 2 * PANEL])
    slab = jnp.exp2(raw[:, 2 * PANEL :] + cs[...])
    scale = jnp.exp2(-SCALE * jnp.sum(points * points, axis=1, keepdims=True))
    ghi, glo = split(panel)
    return jnp.concatenate([ghi, glo, ghi], axis=1), slab, scale


def update_phase(phase, mc):
    panel, slab, scale = phase
    return scale * (slab - dot(panel, mc[...]))


def gather_kernel(
    l_ref, s_ref, p_ref, a_ref, held, res, we, mc, cs, s_v, p_v, a_v, send, recv, loc
):
    z, x, core = place()

    def device(dz, dx, dc):
        return {"col": (((z + dz) % 4) * 2 + (x + dx) % 2) * 2 + (core + dc) % 2}

    partner, across, up, down = device(0, 0, 1), device(0, 1, 0), device(1, 0, 0), device(3, 0, 0)
    ways = {"across": across, "up": up, "down": down}
    barrier = pltpu.get_barrier_semaphore()
    for d in (partner, across, up, down):
        pl.semaphore_signal(barrier, inc=1, device_id=d, device_id_type=MESH)
    own_rows = pl.ds(pl.multiple_of(core * ROWS, ROWS), ROWS)
    local = [
        pltpu.make_async_copy(p_ref, p_v, loc.at[0]),
        pltpu.make_async_copy(s_ref, s_v, loc.at[1]),
        pltpu.make_async_copy(a_ref, a_v, loc.at[2]),
        pltpu.make_async_copy(l_ref, held.at[0, own_rows], loc.at[3]),
    ]
    for n in (0, 1, 3, 2):
        local[n].start()
    pl.semaphore_wait(barrier, 4)

    sends = []

    def go(src, slot, part, target):
        copy = pltpu.make_async_remote_copy(
            src_ref=src,
            dst_ref=held.at[slot, pl.ds(offset((slot, part, 0), core), PIECE)],
            send_sem=send.at[len(sends)],
            recv_sem=recv.at[slot, core, part],
            device_id=target,
            device_id_type=MESH,
        )
        copy.start()
        sends.append(copy)

    def mine(slot, part):
        return held.at[slot, pl.ds(offset((slot, part, 0), core), PIECE)]

    def wait(slot, part, other):
        ref = held.at[slot, pl.ds(offset((slot, part, other), core), PIECE)]
        plane = core if other == 0 else 1 - core
        pltpu.make_async_copy(ref, ref, recv.at[slot, plane, part]).wait()

    def before(i):
        for slot, part, onward in ARRIVALS.get(i, ()):
            wait(slot, part, 0)
            go(mine(slot, part), slot, part, partner)
            for there, way in onward:
                go(mine(slot, part), there, part, ways[way])
        for slot, part, there in LATER.get(i, ()):
            go(mine(slot, part), there, part, down)

    def fetch(unit):
        for slot, part, other in unit:
            if other:
                wait(slot, part, 1)

    for i in range(PARTS):
        ahead = l_ref.at[pl.ds(i * PIECE, PIECE)]
        behind = l_ref.at[pl.ds((PARTS - 1 - i) * PIECE, PIECE)]
        go(ahead, 3, i, up)
        go(behind, 1, PARTS - 1 - i, down)
        go(ahead, 4, i, across)
        go(ahead, 0, i, partner)

    local[0].wait()
    local[1].wait()
    panel = p_v[...].reshape(2 * PANEL, DIM)
    turned = jnp.concatenate([panel.T, s_v[...].T], axis=1)
    scaled = turned * (2.0 * SCALE)
    hi, lo = split(scaled)
    we[...] = jnp.concatenate([hi, hi, lo], axis=0)
    columns = -SCALE * jnp.sum(turned * turned, axis=0, keepdims=True)
    cs[...] = columns[:, 2 * PANEL :]
    local[3].wait()
    pending = []

    def begin(unit):
        pending.append((unit, kernel_phase(rows_of(held, unit, core), we, cs)))

    begin(UNITS_A[0])
    weights = -SCALE * jnp.sum(panel * panel, axis=1, keepdims=True)
    grid = jnp.exp2(dot_full(panel, scaled[:, 2 * PANEL :]) + weights + columns[:, 2 * PANEL :])
    k0, k1 = grid[:PANEL], grid[PANEL:]
    local[2].wait()
    a0, a1 = a_v[0], a_v[1]
    inv0, inv1 = dot_full(a0.T, a0), dot_full(a1.T, a1)
    g10 = jnp.exp2(dot_full(panel[PANEL:], scaled[:, :PANEL]) + weights[PANEL:] + columns[:, :PANEL])
    qt = dot_full(g10, inv0)
    m1 = dot_full(inv1, k1 - dot_full(qt, k0))
    m0 = dot_full(inv0, k0) - dot_full(qt.T, m1)
    scale_rows = jnp.exp2(weights)
    mhi, mlo = split(jnp.concatenate([m0, m1], axis=0) * scale_rows)
    mc[...] = jnp.concatenate([mhi, mhi, mlo], axis=0)
    def finish():
        unit, phase = pending.pop(0)
        out = update_phase(phase, mc)
        for n, piece in enumerate(unit):
            res[piece[0], pl.ds(offset(piece, core), PIECE), :] = out[n * PIECE : (n + 1) * PIECE]

    for i, unit in enumerate(UNITS_A):
        before(i)
        if unit is UNITS_A[-1]:
            before(i + 1)
        fetch(unit)
        if i:
            begin(unit)
            finish()
    finish()
    for unit in UNITS_B:
        fetch(unit)
    for copy in sends:
        copy.wait_send()


def finish_kernel(held, res, we, mc, cs, out, last, sems):
    z, x, core = place()
    copies = []

    def put(src, slot, start, size):
        chip = ((z + slot % 4) % 4) * 2 + (x + slot // 4) % 2
        target = out.at[pl.ds(pl.multiple_of(chip * CHIP + start, PIECE), size)]
        copy = pltpu.make_async_copy(src, target, sems.at[len(copies)])
        copy.start()
        copies.append(copy)

    for slot, part, parts, other in RUNS:
        start = offset((slot, part, other), core)
        put(res.at[slot, pl.ds(start, parts * PIECE)], slot, start, parts * PIECE)
    for slot in DONE:
        put(res.at[slot], slot, 0, CHIP)
    for n, unit in enumerate(UNITS_B):
        phase = kernel_phase(rows_of(held, unit, core), we, cs)
        last[n] = update_phase(phase, mc)
        for m, piece in enumerate(unit):
            put(last.at[n, pl.ds(m * PIECE, PIECE)], piece[0], offset(piece, core), PIECE)
    for copy in copies:
        copy.wait()


def local(landmarks, slab_points, panel_points, inverse_blocks):
    hbm = pl.BlockSpec(memory_space=pltpu.HBM)
    vmem = pl.BlockSpec(memory_space=pltpu.VMEM)
    arguments = [
        pltpu.with_memory_space_constraint(v, pltpu.HBM)
        for v in (landmarks, slab_points, panel_points, inverse_blocks)
    ]
    held, res, we, mc, cs = pl.pallas_call(
        gather_kernel,
        name="gather",
        in_specs=[hbm] * 4,
        out_specs=[vmem] * 5,
        out_shape=[
            pltpu.VMEM((8, CHIP, DIM), F32),
            pltpu.VMEM((8, CHIP, COLS), F32),
            pltpu.VMEM((3 * DIM, 2 * PANEL + COLS), BF16),
            pltpu.VMEM((6 * PANEL, COLS), BF16),
            pltpu.VMEM((1, COLS), F32),
        ],
        scratch_shapes=[
            pltpu.VMEM((COLS, DIM), F32),
            pltpu.VMEM((2, PANEL, DIM), F32),
            pltpu.VMEM((2, PANEL, PANEL), F32),
            pltpu.SemaphoreType.DMA((96,)),
            pltpu.SemaphoreType.DMA((8, 2, PARTS)),
            pltpu.SemaphoreType.DMA((4,)),
        ],
        compiler_params=pltpu.CompilerParams(
            collective_id=0, has_side_effects=True, vmem_limit_bytes=24 << 20
        ),
    )(*arguments)
    return pl.pallas_call(
        finish_kernel,
        name="finish",
        in_specs=[vmem] * 5,
        out_specs=hbm,
        out_shape=jax.ShapeDtypeStruct((8 * CHIP, COLS), F32),
        scratch_shapes=[
            pltpu.VMEM((len(UNITS_B), ROWS, COLS), F32),
            pltpu.SemaphoreType.DMA((32,)),
        ],
        compiler_params=pltpu.CompilerParams(vmem_limit_bytes=24 << 20),
    )(held, res, we, mc, cs)


def solution(mesh):
    in_specs = (P(("row", "col"), None), P("col", None), P(), P())
    return jax.shard_map(
        local, mesh=mesh, in_specs=in_specs, out_specs=P("row", "col"), check_vma=False
    )
```
